32 devices in a mesh: ep: 2 (over core), dp: 16 (over z, y, x).
Axes of the slice: x: 2, y: 2, z: 4, core: 2. Of those that a mesh axis runs over, the one named last changes fastest.
Arguments:
- tokens: bfloat16 [512, 7168], P('dp', 'ep'), may hold values from -6 to 6
- gate_weight: bfloat16 [16, 7168, 1024], P('dp', 'ep'), may hold values from -0.0625 to 0.0625
- up_weight: bfloat16 [16, 7168, 1024], P('dp', 'ep'), may hold values from -0.0625 to 0.0625
- down_weight: bfloat16 [16, 1024, 7168], P('dp', None, 'ep'), may hold values from -0.1875 to 0.1875
- targets: int32 [512, 8], P('dp'), may hold values from 0 to 15, all different within a row; in each aligned block of 32 rows (0 to 31, 32 to 63, ...) at most 32 rows name the same one
- mixing: float32 [512, 8], P('dp'), may hold values from 0.05 to 1
- move_plan: int32 [16], replicated, may hold values from 0 to 15, as said below
Outputs:
- mixed: bfloat16 [512, 7168], P('dp', 'ep')
The draws below stay inside these ranges and needn't reach their ends.
Inputs may be any that keep to these rules, and one draw needn't show every extreme that they name: `targets`: each row names 8 different slots; within the 32 rows of one token group no slot is named more than 32 times, and in some groups one slot exactly 32 times. `move_plan`: every entry is either its own slot or one common source slot; the source serves its own copy; the slot after the source and the slot half of 16 after it (cyclically) always serve the source's copy, and each other slot does so with probability one half.
All inputs are finite; a program needn't handle non-finite values.
Results may differ from the reference program's by a relative error of at most 0.0058.
Values may be sent and summed in bfloat16 or wider, within the bound.
A program may use at most 128 MiB of HBM per device.

```python
import math
import jax
import jax.numpy as jnp
import numpy as np
from jax import lax

D = 7168
FF = 1024
TOP = 8
TOK_G = 32
CAP = 32
TOKENS = 512
N_EP = 2
N_DP = 16


def draw_move_plan(key, part):
    first, second = jax.random.split(jax.random.fold_in(key, 7))
    source_slot = jax.random.randint(first, (), 0, N_DP)
    slots_all = jnp.arange(N_DP, dtype=jnp.int32)
    offset = (slots_all - source_slot) % N_DP
    coins = jax.random.randint(second, (N_DP,), 0, 2)
    served = (offset != 0) & ((coins == 1) | (offset == 1) | (offset == N_DP // 2))
    return jnp.where(served, source_slot, slots_all).astype(jnp.int32)


def steps_of(rng, extent, cuts, smallest, largest):
    factor_of = 1.0
    for position, blocks in cuts:
        draws = jax.random.uniform(jax.random.fold_in(jax.random.fold_in(rng, 6), position), (blocks,), jnp.float32, smallest / len(cuts), largest / len(cuts))
        factor_of = factor_of * jnp.repeat(jnp.exp(draws), extent[position] // blocks).reshape((-1,) + (1,) * (len(extent) - 1 - position))
    return factor_of


def assign_block(stream_key, own, number, rows, count, top, bound, slope):
    ranking = jax.random.permutation(stream_key, count)
    crowded, ordinary = load_shares(count, rows * top, bound, slope, True), load_shares(count, rows * top, bound, slope, False)
    places = jnp.arange(count)

    def named(lengths, turn):
        used = int((lengths > 0).sum())
        fixed = max(1, used // 4)
        passed = fixed + (places - fixed + turn * (used - fixed)) % max(1, count - fixed)
        return jnp.zeros((count,), jnp.int32).at[ranking[jnp.where(places < fixed, places, passed)]].set(jnp.asarray(lengths, jnp.int32))

    lengths = jnp.where(number % 4 == 0, named(crowded, number // 4), named(ordinary, number - number // 4 - 1))
    mixed = jax.random.permutation(jax.random.fold_in(own, 3), count)
    giver, receiver = mixed[0:count // 2 * 2:2], mixed[1:count // 2 * 2:2]
    slack = jnp.minimum(lengths[giver] - 1, bound - lengths[receiver]) // 2
    slack = jnp.where((giver == ranking[0]) | (receiver == ranking[0]) | (lengths[receiver] == 0), 0, jnp.maximum(slack, 0))
    passed = jax.random.randint(jax.random.fold_in(own, 4), (count // 2,), 0, 1 << 20) % (slack + 1)
    lengths = lengths.at[giver].add(-passed).at[receiver].add(passed)
    labels = jnp.searchsorted(jnp.cumsum(lengths), jnp.arange(rows * top), side="right").astype(jnp.int32)
    listing = labels.reshape(top, rows).T
    listing = listing[jax.random.permutation(jax.random.fold_in(own, 1), rows)]
    turn = jax.random.randint(jax.random.fold_in(own, 2), (rows, 1), 0, top)
    return jnp.take_along_axis(listing, (jnp.arange(top)[None, :] + turn) % top, axis=1)


def load_shares(amount, total, reach, slope, full):
    portions = [(1 << 20) // math.isqrt(rank ** slope) + 1 for rank in range(1, amount + 1)]
    largest = reach if full else min(reach, max(-(-total // amount), total * portions[0] // sum(portions)))
    least = 1 if total - largest >= amount - 1 else 0
    given, surplus = [largest] + [least] * (amount - 1), total - largest - least * (amount - 1)
    while surplus > 0:
        free = [i for i in range(1, amount) if given[i] < largest] or [i for i in range(1, amount) if given[i] < reach]
        whole, remaining = sum([portions[i] for i in free]), surplus
        for i in free:
            addition = min(reach - given[i], max(1, remaining * portions[i] // whole), surplus)
            given[i] = given[i] + addition
            surplus = surplus - addition
    return np.array(given)


def bell_draw(rng, shape, deviation, reach, shards=(), held_as=jnp.bfloat16):
    array = jax.random.normal(rng, shape, jnp.float32) * deviation
    if len(shards) > 0:
        array = steps_of(rng, shape, shards, -0.22, 0.18) * array
    return jnp.clip(array, min=-reach, max=reach).astype(held_as)


def setup_inputs(seed: int = 0) -> dict:
    streams_of = jax.random.split(jax.random.key(seed), 8)
    tokens = bell_draw(streams_of[0], (TOKENS, D), 1.0, 6.0, ((0, 16), (1, 2)))
    gate_weight = bell_draw(streams_of[1], (N_DP, D, FF), D ** -0.5, 0.0625, ((0, 16), (1, 2)))
    up_weight = bell_draw(streams_of[2], (N_DP, D, FF), D ** -0.5, 0.0625, ((0, 16), (1, 2)))
    down_weight = bell_draw(streams_of[3], (N_DP, FF, D), FF ** -0.5, 0.1875, ((0, 16), (2, 2)))
    targets_keys = jax.random.split(jax.random.fold_in(streams_of[4], 1), TOKENS // TOK_G)
    targets_turns = jax.random.permutation(jax.random.fold_in(streams_of[4], 3), TOKENS // TOK_G)
    targets = jax.vmap(lambda own, number: assign_block(jax.random.fold_in(streams_of[4], 2), own, number, TOK_G, N_DP, TOP, CAP, 2))(targets_keys, targets_turns).reshape((TOKENS, TOP))
    mixing = jnp.clip(jnp.exp(math.log(1.0) - 2.9957323 * jax.random.uniform(streams_of[5], (TOKENS, TOP), jnp.float32) ** steps_of(streams_of[5], (TOKENS, TOP), ((0, 16),), -0.2, 0.2)), 0.05, 1.0)
    move_plan = draw_move_plan(jax.random.fold_in(streams_of[7], 71), 0)
    return dict(tokens=tokens, gate_weight=gate_weight, up_weight=up_weight, down_weight=down_weight, targets=targets, mixing=mixing, move_plan=move_plan)


def run_expert(rows, gate_cols, up_cols, down_rows):
    count = rows.shape[0]
    width = D // N_EP
    blocks = rows.reshape(count, N_EP, width).astype(jnp.float32)
    gate_blocks = gate_cols.reshape(N_EP, width, FF).astype(jnp.float32)
    up_blocks = up_cols.reshape(N_EP, width, FF).astype(jnp.float32)
    gate = jnp.einsum("nbd,bdf->nf", blocks, gate_blocks)
    up = jnp.einsum("nbd,bdf->nf", blocks, up_blocks)
    hidden = (jax.nn.silu(gate) * up).astype(jnp.bfloat16)
    return jnp.dot(hidden, down_rows, preferred_element_type=jnp.float32).astype(jnp.bfloat16)


def reference(tokens, gate_weight, up_weight, down_weight, targets, mixing, move_plan):
    flat_targets = targets.reshape(-1).astype(jnp.int32)
    flat_mixing = mixing.reshape(-1)
    slots = N_DP * CAP
    places = jnp.arange(slots, dtype=jnp.int32)
    plan = move_plan.astype(jnp.int32)

    def visit(total, group):
        anchor = plan[group].astype(jnp.int32)
        gate_cols = lax.dynamic_index_in_dim(gate_weight, anchor, 0, keepdims=False)
        up_cols = lax.dynamic_index_in_dim(up_weight, anchor, 0, keepdims=False)
        down_rows = lax.dynamic_index_in_dim(down_weight, anchor, 0, keepdims=False)
        chosen = flat_targets == group
        found = jnp.nonzero(chosen, size=slots, fill_value=0)[0].astype(jnp.int32)
        live = places < jnp.sum(chosen.astype(jnp.int32))
        owners = (found // TOP).astype(jnp.int32)
        result = run_expert(tokens[owners], gate_cols, up_cols, down_rows).astype(jnp.float32)
        scale = jnp.where(live, flat_mixing[found], 0.0)
        return total.at[owners].add(result * scale[:, None]), None

    start = jnp.zeros((TOKENS, D), jnp.float32)
    total, unused = lax.scan(visit, start, jnp.arange(N_DP, dtype=jnp.int32))
    return total.astype(jnp.bfloat16)
```

```python
import jax
import jax.numpy as jnp
from jax import lax
from jax.sharding import PartitionSpec as P


def per_device(tokens, gate_weight, up_weight, down_weight, targets, mixing, move_plan):
    groups = lax.axis_size("dp")
    me = lax.axis_index("dp")
    lanes = jnp.arange(groups, dtype=jnp.int32)
    anchors = jnp.sum(
        jnp.where(targets[:, :, None] == lanes, move_plan[None, None, :], 0), axis=2
    )
    share = jnp.sum(
        jnp.where(anchors[:, :, None] == lanes, mixing[:, :, None], 0.0), axis=1
    )
    shares = lax.all_gather(share, "dp", axis=0, tiled=True)
    rows = lax.all_gather(tokens, "dp", axis=0, tiled=True)
    width = rows.shape[0]
    dims = (((0,), (1,)), ((), ()))
    gate_term = lax.dot_general(gate_weight[0], rows, dims, preferred_element_type=jnp.float32)
    up_term = lax.dot_general(up_weight[0], rows, dims, preferred_element_type=jnp.float32)
    summed = lax.psum_scatter(
        jnp.concatenate([gate_term, up_term], axis=1), "ep", scatter_dimension=0, tiled=True
    )
    hidden = (jax.nn.silu(summed[:, :width]) * summed[:, width:]).astype(jnp.bfloat16)
    output = lax.dot_general(
        lax.all_gather(hidden, "ep", axis=0, tiled=True),
        down_weight[0],
        (((0,), (0,)), ((), ())),
        preferred_element_type=jnp.float32,
    )
    scale = jnp.sum(jnp.where(lanes == me, shares, 0.0), axis=1, keepdims=True)
    scaled = output.astype(jnp.bfloat16).astype(jnp.float32) * scale
    mixed = lax.psum_scatter(scaled.astype(jnp.bfloat16), "dp", scatter_dimension=0, tiled=True)
    return mixed.astype(jnp.bfloat16)


def solution(mesh):
    return jax.shard_map(
        per_device,
        mesh=mesh,
        in_specs=(
            P("dp", "ep"),
            P("dp", "ep", None),
            P("dp", "ep", None),
            P("dp", None, "ep"),
            P("dp", None),
            P("dp", None),
            P(),
        ),
        out_specs=P("dp", "ep"),
        check_vma=False,
    )
```

```python
import functools

import jax
import jax.numpy as jnp
from jax import lax
from jax.experimental import pallas as pl
from jax.experimental.pallas import tpu as pltpu
from jax.sharding import PartitionSpec as P

MESH = pl.DeviceIdType.MESH
F32, BF16 = jnp.float32, jnp.bfloat16
PLANE, LINE = 4, 4


def share_of(targets, mixing, move_plan, lanes):
    anchors = jnp.sum(
        jnp.where(targets[:, :, None] == lanes, move_plan[None, None, :], 0), axis=2
    )
    return jnp.sum(jnp.where(anchors[:, :, None] == lanes, mixing[:, :, None], 0.0), axis=1)


def tile_of(extent, largest):
    return next(t for t in (512, 256, 128) if t <= largest and extent % t == 0)


def kernel(
    groups, ext, gate_hbm, up_hbm, down_hbm, out,
    gate, up, down, tok, psend, precv, pown, hid, cont, dsend, dland,
    xsend, ysend, xland, yland, zsend, zland, acc,
    wsem, own_sem, col_s, col_r, ag_s, ag_r, ep_s, ep_r, rs_s, rs_r, z_s, z_r,
):
    me = lax.axis_index("dp")
    core = lax.axis_index("ep")
    rows = ext.shape[0]
    half = rows // 2
    wide = gate.shape[0]
    keep = psend.shape[2] // 2
    block = PLANE * rows
    z = me // PLANE
    j = me % PLANE
    y, x = j // 2, j % 2
    jx, jy, jd = y * 2 + 1 - x, (1 - y) * 2 + x, (1 - y) * 2 + 1 - x
    dx, dy = z * PLANE + jx, z * PLANE + jy
    top = z // 2
    inner = z + top * (LINE - 1 - 2 * z)
    mirrored = (inner, 1 - inner, 2, 3)
    plane = [q + top * (LINE - 1 - 2 * q) for q in mirrored]

    weight_copies = [
        pltpu.make_async_copy(gate_hbm, gate, wsem.at[0]),
        pltpu.make_async_copy(up_hbm, up, wsem.at[1]),
        pltpu.make_async_copy(down_hbm, down, wsem.at[2]),
    ]
    for c in weight_copies:
        c.start()

    def at_rows(slot):
        return pl.ds(pl.multiple_of(slot * rows, rows), rows)

    def at_half(slot, h):
        return pl.ds(pl.multiple_of(slot * rows + h * half, half), half)

    own_copy = pltpu.make_async_copy(ext, tok.at[at_rows(me)], own_sem.at[0])
    own_copy.start()

    peers = [plane[i] * PLANE + j for i in range(1, LINE)]
    barrier = pltpu.get_barrier_semaphore()
    for d in [dx, dy] + peers:
        pl.semaphore_signal(barrier, inc=1, device_id={"dp": d}, device_id_type=MESH)
    pl.semaphore_signal(barrier, inc=1, device_id={"ep": 1 - core}, device_id_type=MESH)
    pl.semaphore_wait(barrier, len(peers) + 3)

    started = []

    def send(src, dst, ss, rs, device):
        c = pltpu.make_async_remote_copy(
            src_ref=src, dst_ref=dst, send_sem=ss, recv_sem=rs,
            device_id=device, device_id_type=MESH,
        )
        c.start()
        started.append(c)

    def landed(dst, ss, rs, device):
        pltpu.make_async_remote_copy(
            src_ref=dst, dst_ref=dst, send_sem=ss, recv_sem=rs,
            device_id=device, device_id_type=MESH,
        ).wait_recv()

    X, Y, E = {"dp": dx}, {"dp": dy}, {"ep": 1 - core}

    def spread_xy(s):
        src = ext if s == 0 else tok.at[at_rows(plane[s] * PLANE + j)]
        dst = tok.at[at_rows(plane[s] * PLANE + j)]
        send(src, dst, ag_s.at[0, s], ag_r.at[0, s], X)
        send(src, dst, ag_s.at[1, s], ag_r.at[1, s], Y)

    def column_forward(s):
        landed(tok.at[at_rows(plane[s] * PLANE + j)], col_s.at[s - 1], col_r.at[plane[s]], X)
        spread_xy(s)

    def half_forward(s):
        base = plane[s] * PLANE
        landed(tok.at[at_rows(base + jx)], ag_s.at[0, s], ag_r.at[0, s], X)
        part = tok.at[at_half(base + jx, 0)]
        send(part, part, ag_s.at[2, s], ag_r.at[2, s], Y)
        landed(tok.at[at_rows(base + jy)], ag_s.at[1, s], ag_r.at[1, s], Y)
        part = tok.at[at_half(base + jy, 1)]
        send(part, part, ag_s.at[3, s], ag_r.at[3, s], X)

    def diag_wait(s):
        base = plane[s] * PLANE
        landed(tok.at[at_half(base + jd, 0)], ag_s.at[2, s], ag_r.at[2, s], Y)
        landed(tok.at[at_half(base + jd, 1)], ag_s.at[3, s], ag_r.at[3, s], X)

    gtile = tile_of(keep, 256)

    def project(s, side, put):
        here = pl.ds(pl.multiple_of(plane[s] * block, block), block)

        @pl.loop(0, keep // gtile)
        def _(n):
            off = pl.multiple_of(n * gtile, gtile)
            src = pl.ds(pl.multiple_of(side * keep + off, gtile), gtile)
            lhs = tok[here, pl.ds(0, wide)]
            put[:, pl.ds(off, gtile)] = jnp.dot(lhs, gate[:, src], preferred_element_type=F32)
            put[:, pl.ds(pl.multiple_of(keep + off, gtile), gtile)] = jnp.dot(
                lhs, up[:, src], preferred_element_type=F32
            )

    def hide(s):
        landed(precv.at[s], ep_s.at[0, s], ep_r.at[0, s], E)
        g = pown[:, pl.ds(0, keep)] + precv[s, :, pl.ds(0, keep)]
        u = pown[:, pl.ds(keep, keep)] + precv[s, :, pl.ds(keep, keep)]
        hid[s, core] = (g / (1.0 + jnp.exp(-g)) * u).astype(BF16)
        send(hid.at[s, core], hid.at[s, core], ep_s.at[1, s], ep_r.at[1, s], E)

    dtile = tile_of(wide, 512)

    def lower(s):
        here = pl.ds(pl.multiple_of(plane[s] * block, block), block)
        packed = tok[here, pl.ds(wide, tok.shape[1] - wide)].astype(F32)
        lane = lax.broadcasted_iota(jnp.int32, packed.shape, 1)
        share = jnp.sum(jnp.where(lane % groups == me, packed, 0.0), axis=1, keepdims=True)
        landed(hid.at[s, 1 - core], ep_s.at[1, s], ep_r.at[1, s], E)

        @pl.loop(0, wide // dtile)
        def _(n):
            cols = pl.ds(pl.multiple_of(n * dtile, dtile), dtile)
            e = jnp.dot(hid[s, 0], down[pl.ds(0, keep), cols], preferred_element_type=F32)
            e += jnp.dot(hid[s, 1], down[pl.ds(keep, keep), cols], preferred_element_type=F32)
            cont[s, :, cols] = e.astype(BF16).astype(F32) * share

        dsend[s] = cont[s, at_rows(jd)].astype(BF16)
        send(dsend.at[s, pl.ds(0, half)], dland.at[s, pl.ds(0, half)], rs_s.at[0, s], rs_r.at[0, s], Y)
        send(dsend.at[s, pl.ds(half, half)], dland.at[s, pl.ds(half, half)], rs_s.at[1, s], rs_r.at[1, s], X)

    def reduce_first(s):
        landed(dland.at[s, pl.ds(0, half)], rs_s.at[0, s], rs_r.at[0, s], Y)
        xsend[s, pl.ds(0, half)] = (
            cont[s, at_half(jx, 0)] + dland[s, pl.ds(0, half)].astype(F32)
        ).astype(BF16)
        xsend[s, pl.ds(half, half)] = cont[s, at_half(jx, 1)].astype(BF16)
        send(xsend.at[s], xland.at[s], rs_s.at[2, s], rs_r.at[2, s], X)
        landed(dland.at[s, pl.ds(half, half)], rs_s.at[1, s], rs_r.at[1, s], X)
        ysend[s, pl.ds(0, half)] = cont[s, at_half(jy, 0)].astype(BF16)
        ysend[s, pl.ds(half, half)] = (
            cont[s, at_half(jy, 1)] + dland[s, pl.ds(half, half)].astype(F32)
        ).astype(BF16)
        send(ysend.at[s], yland.at[s], rs_s.at[3, s], rs_r.at[3, s], Y)

    def reduce_second(s):
        landed(xland.at[s], rs_s.at[2, s], rs_r.at[2, s], X)
        landed(yland.at[s], rs_s.at[3, s], rs_r.at[3, s], Y)
        total = cont[s, at_rows(j)] + xland[s].astype(F32) + yland[s].astype(F32)
        if s == 0:
            acc[...] = total
        else:
            zsend[s] = total.astype(BF16)
            send(zsend.at[s], zland.at[z], z_s.at[s], z_r.at[z], {"dp": peers[s - 1]})

    spread_xy(0)
    for i in range(1, LINE):
        send(ext, tok.at[at_rows(me)], col_s.at[i - 1], col_r.at[z], {"dp": peers[i - 1]})
    half_forward(0)
    column_forward(1)
    own_copy.wait()
    for s in range(LINE):
        diag_wait(s)
        if s == 0:
            weight_copies[0].wait()
            weight_copies[1].wait()
        project(s, 1 - core, psend.at[s])
        send(psend.at[s], precv.at[s], ep_s.at[0, s], ep_r.at[0, s], E)
        project(s, core, pown)
        hide(s)
        if s + 1 < LINE:
            half_forward(s + 1)
        if s + 2 < LINE:
            column_forward(s + 2)
        if s >= 1:
            reduce_first(s - 1)
        if s >= 2:
            reduce_second(s - 2)
        if s == 0:
            weight_copies[2].wait()
        lower(s)
    reduce_first(LINE - 1)
    reduce_second(LINE - 2)
    reduce_second(LINE - 1)
    total = acc[...]
    for s in range(1, LINE):
        landed(zland.at[plane[s]], z_s.at[s], z_r.at[plane[s]], X)
        total += zland[plane[s]].astype(F32)
    out[...] = total.astype(BF16)
    for c in started:
        c.wait_send()


def fused(tokens, gate_weight, up_weight, down_weight, targets, mixing, move_plan):
    groups = lax.axis_size("dp")
    rows, wide = tokens.shape
    lanes = jnp.arange(groups, dtype=jnp.int32)
    share = share_of(targets, mixing, move_plan, lanes)
    high = lax.reduce_precision(share, 8, 7)
    middle = lax.reduce_precision(share - high, 8, 7)
    low = share - high - middle
    pad = -(3 * groups) % 128
    ext = jnp.concatenate(
        [tokens, high.astype(BF16), middle.astype(BF16), low.astype(BF16), jnp.zeros((rows, pad), BF16)],
        axis=1,
    )
    full = gate_weight.shape[2]
    keep = full // lax.axis_size("ep")
    block = PLANE * rows
    VM, DMA = pltpu.VMEM, pltpu.SemaphoreType.DMA
    return pl.pallas_call(
        functools.partial(kernel, groups),
        out_shape=jax.ShapeDtypeStruct((rows, wide), BF16),
        in_specs=[pl.BlockSpec(memory_space=pltpu.VMEM)] + [pl.BlockSpec(memory_space=pl.ANY)] * 3,
        out_specs=pl.BlockSpec(memory_space=pltpu.VMEM),
        scratch_shapes=[
            VM((wide, full), BF16), VM((wide, full), BF16), VM((full, wide), BF16),
            VM((groups * rows, ext.shape[1]), BF16),
            VM((LINE, block, 2 * keep), F32), VM((LINE, block, 2 * keep), F32),
            VM((block, 2 * keep), F32), VM((LINE, 2, block, keep), BF16),
            VM((LINE, block, wide), F32),
            VM((LINE, rows, wide), BF16), VM((LINE, rows, wide), BF16),
            VM((LINE, rows, wide), BF16), VM((LINE, rows, wide), BF16),
            VM((LINE, rows, wide), BF16), VM((LINE, rows, wide), BF16),
            VM((LINE, rows, wide), BF16), VM((LINE, rows, wide), BF16),
            VM((rows, wide), F32),
            DMA((3,)), DMA((1,)), DMA((LINE - 1,)), DMA((LINE,)),
            DMA((4, LINE)), DMA((4, LINE)), DMA((2, LINE)), DMA((2, LINE)),
            DMA((4, LINE)), DMA((4, LINE)), DMA((LINE,)), DMA((LINE,)),
        ],
        compiler_params=pltpu.CompilerParams(
            collective_id=0, has_side_effects=True, vmem_limit_bytes=63 * 1024 * 1024
        ),
    )(ext, gate_weight[0], up_weight[0], down_weight[0])


def plain(tokens, gate_weight, up_weight, down_weight, targets, mixing, move_plan):
    groups = lax.axis_size("dp")
    me = lax.axis_index("dp")
    lanes = jnp.arange(groups, dtype=jnp.int32)
    share = share_of(targets, mixing, move_plan, lanes)
    shares = lax.all_gather(share, "dp", axis=0, tiled=True)
    rows = lax.all_gather(tokens, "dp", axis=0, tiled=True)
    width = rows.shape[0]
    dims = (((0,), (1,)), ((), ()))
    gate_term = lax.dot_general(gate_weight[0], rows, dims, preferred_element_type=F32)
    up_term = lax.dot_general(up_weight[0], rows, dims, preferred_element_type=F32)
    summed = lax.psum_scatter(
        jnp.concatenate([gate_term, up_term], axis=1), "ep", scatter_dimension=0, tiled=True
    )
    hidden = (jax.nn.silu(summed[:, :width]) * summed[:, width:]).astype(BF16)
    output = lax.dot_general(
        lax.all_gather(hidden, "ep", axis=0, tiled=True),
        down_weight[0],
        (((0,), (0,)), ((), ())),
        preferred_element_type=F32,
    )
    scale = jnp.sum(jnp.where(lanes == me, shares, 0.0), axis=1, keepdims=True)
    scaled = output.astype(BF16).astype(F32) * scale
    return lax.psum_scatter(scaled.astype(BF16), "dp", scatter_dimension=0, tiled=True)


def solution(mesh):
    small = mesh.shape["dp"] == PLANE * LINE and mesh.shape["ep"] == 2
    return jax.shard_map(
        fused if small else plain,
        mesh=mesh,
        in_specs=(
            P("dp", "ep"),
            P("dp", "ep", None),
            P("dp", "ep", None),
            P("dp", None, "ep"),
            P("dp", None),
            P("dp", None),
            P(),
        ),
        out_specs=P("dp", "ep"),
        check_vma=False,
    )
```

```python
import functools

import jax
import jax.numpy as jnp
from jax import lax
from jax.experimental import pallas as pl
from jax.experimental.pallas import tpu as pltpu
from jax.sharding import PartitionSpec as P

MESH = pl.DeviceIdType.MESH
F32, BF16 = jnp.float32, jnp.bfloat16
PLANE, LINE = 4, 4


def share_of(targets, mixing, move_plan, lanes):
    anchors = jnp.sum(
        jnp.where(targets[:, :, None] == lanes, move_plan[None, None, :], 0), axis=2
    )
    return jnp.sum(jnp.where(anchors[:, :, None] == lanes, mixing[:, :, None], 0.0), axis=1)


def tile_of(extent, largest):
    return next(t for t in (512, 256, 128) if t <= largest and extent % t == 0)


def kernel(
    groups, ext, gate_hbm, up_hbm, down_hbm, out,
    gate, up, down, tok, psend, precv, pown, hid, cont, dsend, dland,
    xsend, ysend, xland, yland, zsend, zland, acc,
    wsem, own_sem, col_s, col_r, ag_s, ag_r, ep_s, ep_r, rs_s, rs_r, z_s, z_r,
):
    me = lax.axis_index("dp")
    core = lax.axis_index("ep")
    rows = ext.shape[0]
    half = rows // 2
    wide = gate.shape[0]
    keep = psend.shape[2] // 2
    block = PLANE * rows
    z = me // PLANE
    j = me % PLANE
    y, x = j // 2, j % 2
    jx, jy, jd = y * 2 + 1 - x, (1 - y) * 2 + x, (1 - y) * 2 + 1 - x
    dx, dy = z * PLANE + jx, z * PLANE + jy
    top = z // 2
    inner = z + top * (LINE - 1 - 2 * z)
    mirrored = (inner, 1 - inner, 2, 3)
    plane = [q + top * (LINE - 1 - 2 * q) for q in mirrored]

    weight_copies = [
        pltpu.make_async_copy(gate_hbm, gate, wsem.at[0]),
        pltpu.make_async_copy(up_hbm, up, wsem.at[1]),
        pltpu.make_async_copy(down_hbm, down, wsem.at[2]),
    ]
    def at_rows(slot):
        return pl.ds(pl.multiple_of(slot * rows, rows), rows)

    def at_half(slot, h):
        return pl.ds(pl.multiple_of(slot * rows + h * half, half), half)

    own_copy = pltpu.make_async_copy(ext, tok.at[at_rows(me)], own_sem.at[0])
    own_copy.start()

    peers = [plane[i] * PLANE + j for i in range(1, LINE)]
    barrier = pltpu.get_barrier_semaphore()
    for d in [dx, dy] + peers:
        pl.semaphore_signal(barrier, inc=1, device_id={"dp": d}, device_id_type=MESH)
    pl.semaphore_signal(barrier, inc=1, device_id={"ep": 1 - core}, device_id_type=MESH)
    pl.semaphore_wait(barrier, len(peers) + 3)

    started = []

    def send(src, dst, ss, rs, device):
        c = pltpu.make_async_remote_copy(
            src_ref=src, dst_ref=dst, send_sem=ss, recv_sem=rs,
            device_id=device, device_id_type=MESH,
        )
        c.start()
        started.append(c)

    def landed(dst, ss, rs, device):
        pltpu.make_async_remote_copy(
            src_ref=dst, dst_ref=dst, send_sem=ss, recv_sem=rs,
            device_id=device, device_id_type=MESH,
        ).wait_recv()

    X, Y, E = {"dp": dx}, {"dp": dy}, {"ep": 1 - core}

    def spread_xy(s):
        src = ext if s == 0 else tok.at[at_rows(plane[s] * PLANE + j)]
        dst = tok.at[at_rows(plane[s] * PLANE + j)]
        send(src, dst, ag_s.at[0, s], ag_r.at[0, s], X)
        send(src, dst, ag_s.at[1, s], ag_r.at[1, s], Y)

    def column_forward(s):
        landed(tok.at[at_rows(plane[s] * PLANE + j)], col_s.at[s - 1], col_r.at[plane[s]], X)
        spread_xy(s)

    def half_forward(s):
        base = plane[s] * PLANE
        landed(tok.at[at_rows(base + jx)], ag_s.at[0, s], ag_r.at[0, s], X)
        part = tok.at[at_half(base + jx, 0)]
        send(part, part, ag_s.at[2, s], ag_r.at[2, s], Y)
        landed(tok.at[at_rows(base + jy)], ag_s.at[1, s], ag_r.at[1, s], Y)
        part = tok.at[at_half(base + jy, 1)]
        send(part, part, ag_s.at[3, s], ag_r.at[3, s], X)

    def diag_wait(s):
        base = plane[s] * PLANE
        landed(tok.at[at_half(base + jd, 0)], ag_s.at[2, s], ag_r.at[2, s], Y)
        landed(tok.at[at_half(base + jd, 1)], ag_s.at[3, s], ag_r.at[3, s], X)

    gtile = tile_of(keep, 512)

    def project(s, side, put):
        here = pl.ds(pl.multiple_of(plane[s] * block, block), block)

        @pl.loop(0, keep // gtile)
        def _(n):
            off = pl.multiple_of(n * gtile, gtile)
            src = pl.ds(pl.multiple_of(side * keep + off, gtile), gtile)
            lhs = tok[here, pl.ds(0, wide)]
            put[:, pl.ds(off, gtile)] = jnp.dot(lhs, gate[:, src], preferred_element_type=F32)
            put[:, pl.ds(pl.multiple_of(keep + off, gtile), gtile)] = jnp.dot(
                lhs, up[:, src], preferred_element_type=F32
            )

    def hide(s):
        landed(precv.at[s], ep_s.at[0, s], ep_r.at[0, s], E)
        g = pown[:, pl.ds(0, keep)] + precv[s, :, pl.ds(0, keep)]
        u = pown[:, pl.ds(keep, keep)] + precv[s, :, pl.ds(keep, keep)]
        hid[s, core] = (g / (1.0 + jnp.exp(-g)) * u).astype(BF16)
        send(hid.at[s, core], hid.at[s, core], ep_s.at[1, s], ep_r.at[1, s], E)

    dtile = tile_of(wide, 512)

    def lower(s):
        here = pl.ds(pl.multiple_of(plane[s] * block, block), block)
        packed = tok[here, pl.ds(wide, tok.shape[1] - wide)].astype(F32)
        lane = lax.broadcasted_iota(jnp.int32, packed.shape, 1)
        share = jnp.sum(jnp.where(lane % groups == me, packed, 0.0), axis=1, keepdims=True)
        landed(hid.at[s, 1 - core], ep_s.at[1, s], ep_r.at[1, s], E)

        @pl.loop(0, wide // dtile)
        def _(n):
            cols = pl.ds(pl.multiple_of(n * dtile, dtile), dtile)
            e = jnp.dot(hid[s, 0], down[pl.ds(0, keep), cols], preferred_element_type=F32)
            e += jnp.dot(hid[s, 1], down[pl.ds(keep, keep), cols], preferred_element_type=F32)
            cont[s, :, cols] = e.astype(BF16).astype(F32) * share

        dsend[s] = cont[s, at_rows(jd)].astype(BF16)
        send(dsend.at[s, pl.ds(0, half)], dland.at[s, pl.ds(0, half)], rs_s.at[0, s], rs_r.at[0, s], Y)
        send(dsend.at[s, pl.ds(half, half)], dland.at[s, pl.ds(half, half)], rs_s.at[1, s], rs_r.at[1, s], X)

    def reduce_first(s):
        landed(dland.at[s, pl.ds(0, half)], rs_s.at[0, s], rs_r.at[0, s], Y)
        xsend[s, pl.ds(0, half)] = (
            cont[s, at_half(jx, 0)] + dland[s, pl.ds(0, half)].astype(F32)
        ).astype(BF16)
        xsend[s, pl.ds(half, half)] = cont[s, at_half(jx, 1)].astype(BF16)
        send(xsend.at[s], xland.at[s], rs_s.at[2, s], rs_r.at[2, s], X)
        landed(dland.at[s, pl.ds(half, half)], rs_s.at[1, s], rs_r.at[1, s], X)
        ysend[s, pl.ds(0, half)] = cont[s, at_half(jy, 0)].astype(BF16)
        ysend[s, pl.ds(half, half)] = (
            cont[s, at_half(jy, 1)] + dland[s, pl.ds(half, half)].astype(F32)
        ).astype(BF16)
        send(ysend.at[s], yland.at[s], rs_s.at[3, s], rs_r.at[3, s], Y)

    def reduce_second(s):
        landed(xland.at[s], rs_s.at[2, s], rs_r.at[2, s], X)
        landed(yland.at[s], rs_s.at[3, s], rs_r.at[3, s], Y)
        total = cont[s, at_rows(j)] + xland[s].astype(F32) + yland[s].astype(F32)
        if s == 0:
            acc[...] = total
        else:
            zsend[s] = total.astype(BF16)
            send(zsend.at[s], zland.at[z], z_s.at[s], z_r.at[z], {"dp": peers[s - 1]})

    spread_xy(0)
    for i in range(1, LINE):
        send(ext, tok.at[at_rows(me)], col_s.at[i - 1], col_r.at[z], {"dp": peers[i - 1]})
    for c in weight_copies:
        c.start()
    half_forward(0)
    column_forward(1)
    half_forward(1)
    column_forward(2)
    own_copy.wait()
    order = list(range(1, LINE)) + [0]
    for k, s in enumerate(order):
        diag_wait(s)
        if k == 0:
            weight_copies[0].wait()
            weight_copies[1].wait()
        project(s, 1 - core, psend.at[s])
        send(psend.at[s], precv.at[s], ep_s.at[0, s], ep_r.at[0, s], E)
        project(s, core, pown)
        hide(s)
        if k + 2 < LINE:
            half_forward(k + 2)
        if k + 3 < LINE:
            column_forward(k + 3)
        if k >= 1:
            reduce_first(order[k - 1])
        if k >= 2:
            reduce_second(order[k - 2])
        if k == 0:
            weight_copies[2].wait()
        lower(s)
    reduce_first(order[-1])
    reduce_second(order[-2])
    reduce_second(order[-1])
    total = acc[...]
    for s in range(1, LINE):
        landed(zland.at[plane[s]], z_s.at[s], z_r.at[plane[s]], X)
        total += zland[plane[s]].astype(F32)
    out[...] = total.astype(BF16)
    for c in started:
        c.wait_send()


def fused(tokens, gate_weight, up_weight, down_weight, targets, mixing, move_plan):
    groups = lax.axis_size("dp")
    rows, wide = tokens.shape
    lanes = jnp.arange(groups, dtype=jnp.int32)
    share = share_of(targets, mixing, move_plan, lanes)
    high = lax.reduce_precision(share, 8, 7)
    middle = lax.reduce_precision(share - high, 8, 7)
    low = share - high - middle
    pad = -(3 * groups) % 128
    ext = jnp.concatenate(
        [tokens, high.astype(BF16), middle.astype(BF16), low.astype(BF16), jnp.zeros((rows, pad), BF16)],
        axis=1,
    )
    full = gate_weight.shape[2]
    keep = full // lax.axis_size("ep")
    block = PLANE * rows
    VM, DMA = pltpu.VMEM, pltpu.SemaphoreType.DMA
    return pl.pallas_call(
        functools.partial(kernel, groups),
        out_shape=jax.ShapeDtypeStruct((rows, wide), BF16),
        in_specs=[pl.BlockSpec(memory_space=pltpu.VMEM)] + [pl.BlockSpec(memory_space=pl.ANY)] * 3,
        out_specs=pl.BlockSpec(memory_space=pltpu.VMEM),
        scratch_shapes=[
            VM((wide, full), BF16), VM((wide, full), BF16), VM((full, wide), BF16),
            VM((groups * rows, ext.shape[1]), BF16),
            VM((LINE, block, 2 * keep), F32), VM((LINE, block, 2 * keep), F32),
            VM((block, 2 * keep), F32), VM((LINE, 2, block, keep), BF16),
            VM((LINE, block, wide), F32),
            VM((LINE, rows, wide), BF16), VM((LINE, rows, wide), BF16),
            VM((LINE, rows, wide), BF16), VM((LINE, rows, wide), BF16),
            VM((LINE, rows, wide), BF16), VM((LINE, rows, wide), BF16),
            VM((LINE, rows, wide), BF16), VM((LINE, rows, wide), BF16),
            VM((rows, wide), F32),
            DMA((3,)), DMA((1,)), DMA((LINE - 1,)), DMA((LINE,)),
            DMA((4, LINE)), DMA((4, LINE)), DMA((2, LINE)), DMA((2, LINE)),
            DMA((4, LINE)), DMA((4, LINE)), DMA((LINE,)), DMA((LINE,)),
        ],
        compiler_params=pltpu.CompilerParams(
            collective_id=0, has_side_effects=True, vmem_limit_bytes=63 * 1024 * 1024
        ),
    )(ext, gate_weight[0], up_weight[0], down_weight[0])


def plain(tokens, gate_weight, up_weight, down_weight, targets, mixing, move_plan):
    groups = lax.axis_size("dp")
    me = lax.axis_index("dp")
    lanes = jnp.arange(groups, dtype=jnp.int32)
    share = share_of(targets, mixing, move_plan, lanes)
    shares = lax.all_gather(share, "dp", axis=0, tiled=True)
    rows = lax.all_gather(tokens, "dp", axis=0, tiled=True)
    width = rows.shape[0]
    dims = (((0,), (1,)), ((), ()))
    gate_term = lax.dot_general(gate_weight[0], rows, dims, preferred_element_type=F32)
    up_term = lax.dot_general(up_weight[0], rows, dims, preferred_element_type=F32)
    summed = lax.psum_scatter(
        jnp.concatenate([gate_term, up_term], axis=1), "ep", scatter_dimension=0, tiled=True
    )
    hidden = (jax.nn.silu(summed[:, :width]) * summed[:, width:]).astype(BF16)
    output = lax.dot_general(
        lax.all_gather(hidden, "ep", axis=0, tiled=True),
        down_weight[0],
        (((0,), (0,)), ((), ())),
        preferred_element_type=F32,
    )
    scale = jnp.sum(jnp.where(lanes == me, shares, 0.0), axis=1, keepdims=True)
    scaled = output.astype(BF16).astype(F32) * scale
    return lax.psum_scatter(scaled.astype(BF16), "dp", scatter_dimension=0, tiled=True)


def solution(mesh):
    small = mesh.shape["dp"] == PLANE * LINE and mesh.shape["ep"] == 2
    return jax.shard_map(
        fused if small else plain,
        mesh=mesh,
        in_specs=(
            P("dp", "ep"),
            P("dp", "ep", None),
            P("dp", "ep", None),
            P("dp", None, "ep"),
            P("dp", None),
            P("dp", None),
            P(),
        ),
        out_specs=P("dp", "ep"),
        check_vma=False,
    )
```

```python
import functools

import jax
import jax.numpy as jnp
from jax import lax
from jax.experimental import pallas as pl
from jax.experimental.pallas import tpu as pltpu
from jax.sharding import PartitionSpec as P

MESH = pl.DeviceIdType.MESH
F32, BF16 = jnp.float32, jnp.bfloat16
PLANE, LINE = 4, 4


def share_of(targets, mixing, move_plan, lanes):
    anchors = jnp.sum(
        jnp.where(targets[:, :, None] == lanes, move_plan[None, None, :], 0), axis=2
    )
    return jnp.sum(jnp.where(anchors[:, :, None] == lanes, mixing[:, :, None], 0.0), axis=1)


def tile_of(extent, largest):
    return next(t for t in (512, 256, 128) if t <= largest and extent % t == 0)


def kernel(
    groups, ext, gate_hbm, up_hbm, down_hbm, out,
    gate, up, down, tok, psend, precv, pown, hid, cont, dsend, dland,
    xsend, ysend, xland, yland, zsend, zland, acc,
    wsem, own_sem, col_s, col_r, ag_s, ag_r, ep_s, ep_r, rs_s, rs_r, z_s, z_r,
):
    me = lax.axis_index("dp")
    core = lax.axis_index("ep")
    rows = ext.shape[0]
    half = rows // 2
    wide = gate.shape[0]
    keep = psend.shape[2] // 2
    block = PLANE * rows
    z = me // PLANE
    j = me % PLANE
    y, x = j // 2, j % 2
    jx, jy, jd = y * 2 + 1 - x, (1 - y) * 2 + x, (1 - y) * 2 + 1 - x
    dx, dy = z * PLANE + jx, z * PLANE + jy
    top = z // 2
    inner = z + top * (LINE - 1 - 2 * z)
    mirrored = (inner, 1 - inner, 2, 3)
    plane = [q + top * (LINE - 1 - 2 * q) for q in mirrored]

    weight_copies = [
        pltpu.make_async_copy(gate_hbm, gate, wsem.at[0]),
        pltpu.make_async_copy(up_hbm, up, wsem.at[1]),
        pltpu.make_async_copy(down_hbm, down, wsem.at[2]),
    ]
    def at_rows(slot):
        return pl.ds(pl.multiple_of(slot * rows, rows), rows)

    def at_half(slot, h):
        return pl.ds(pl.multiple_of(slot * rows + h * half, half), half)

    own_copy = pltpu.make_async_copy(ext, tok.at[at_rows(me)], own_sem.at[0])
    own_copy.start()

    peers = [plane[i] * PLANE + j for i in range(1, LINE)]
    barrier = pltpu.get_barrier_semaphore()
    for d in [dx, dy] + peers:
        pl.semaphore_signal(barrier, inc=1, device_id={"dp": d}, device_id_type=MESH)
    pl.semaphore_signal(barrier, inc=1, device_id={"ep": 1 - core}, device_id_type=MESH)
    pl.semaphore_wait(barrier, len(peers) + 3)

    started = []

    def send(src, dst, ss, rs, device):
        c = pltpu.make_async_remote_copy(
            src_ref=src, dst_ref=dst, send_sem=ss, recv_sem=rs,
            device_id=device, device_id_type=MESH,
        )
        c.start()
        started.append(c)

    def landed(dst, ss, rs, device):
        pltpu.make_async_remote_copy(
            src_ref=dst, dst_ref=dst, send_sem=ss, recv_sem=rs,
            device_id=device, device_id_type=MESH,
        ).wait_recv()

    X, Y, E = {"dp": dx}, {"dp": dy}, {"ep": 1 - core}

    def spread_xy(s):
        src = ext if s == 0 else tok.at[at_rows(plane[s] * PLANE + j)]
        dst = tok.at[at_rows(plane[s] * PLANE + j)]
        send(src, dst, ag_s.at[0, s], ag_r.at[0, s], X)
        send(src, dst, ag_s.at[1, s], ag_r.at[1, s], Y)

    def column_forward(s):
        landed(tok.at[at_rows(plane[s] * PLANE + j)], col_s.at[s - 1], col_r.at[plane[s]], X)
        spread_xy(s)

    def half_forward(s):
        base = plane[s] * PLANE
        landed(tok.at[at_rows(base + jx)], ag_s.at[0, s], ag_r.at[0, s], X)
        part = tok.at[at_half(base + jx, 0)]
        send(part, part, ag_s.at[2, s], ag_r.at[2, s], Y)
        landed(tok.at[at_rows(base + jy)], ag_s.at[1, s], ag_r.at[1, s], Y)
        part = tok.at[at_half(base + jy, 1)]
        send(part, part, ag_s.at[3, s], ag_r.at[3, s], X)

    def diag_wait(s):
        base = plane[s] * PLANE
        landed(tok.at[at_half(base + jd, 0)], ag_s.at[2, s], ag_r.at[2, s], Y)
        landed(tok.at[at_half(base + jd, 1)], ag_s.at[3, s], ag_r.at[3, s], X)

    gtile = tile_of(keep, 512)

    def project(s, side, put):
        here = pl.ds(pl.multiple_of(plane[s] * block, block), block)

        @pl.loop(0, keep // gtile)
        def _(n):
            off = pl.multiple_of(n * gtile, gtile)
            src = pl.ds(pl.multiple_of(side * keep + off, gtile), gtile)
            lhs = tok[here, pl.ds(0, wide)]
            put[:, pl.ds(off, gtile)] = jnp.dot(lhs, gate[:, src], preferred_element_type=F32)
            put[:, pl.ds(pl.multiple_of(keep + off, gtile), gtile)] = jnp.dot(
                lhs, up[:, src], preferred_element_type=F32
            )

    def hide(s):
        landed(precv.at[s], ep_s.at[0, s], ep_r.at[0, s], E)
        g = pown[:, pl.ds(0, keep)] + precv[s, :, pl.ds(0, keep)]
        u = pown[:, pl.ds(keep, keep)] + precv[s, :, pl.ds(keep, keep)]
        hid[s, core] = (g / (1.0 + jnp.exp(-g)) * u).astype(BF16)
        send(hid.at[s, core], hid.at[s, core], ep_s.at[1, s], ep_r.at[1, s], E)

    dtile = tile_of(wide, 512)

    def lower(s):
        here = pl.ds(pl.multiple_of(plane[s] * block, block), block)
        packed = tok[here, pl.ds(wide, tok.shape[1] - wide)].astype(F32)
        lane = lax.broadcasted_iota(jnp.int32, packed.shape, 1)
        share = jnp.sum(jnp.where(lane % groups == me, packed, 0.0), axis=1, keepdims=True)
        landed(hid.at[s, 1 - core], ep_s.at[1, s], ep_r.at[1, s], E)

        @pl.loop(0, wide // dtile)
        def _(n):
            cols = pl.ds(pl.multiple_of(n * dtile, dtile), dtile)
            e = jnp.dot(hid[s, 0], down[pl.ds(0, keep), cols], preferred_element_type=F32)
            e += jnp.dot(hid[s, 1], down[pl.ds(keep, keep), cols], preferred_element_type=F32)
            cont[s, :, cols] = e.astype(BF16).astype(F32) * share

        dsend[s] = cont[s, at_rows(jd)].astype(BF16)
        send(dsend.at[s, pl.ds(0, half)], dland.at[s, pl.ds(0, half)], rs_s.at[0, s], rs_r.at[0, s], Y)
        send(dsend.at[s, pl.ds(half, half)], dland.at[s, pl.ds(half, half)], rs_s.at[1, s], rs_r.at[1, s], X)
        xsend[s, pl.ds(half, half)] = cont[s, at_half(jx, 1)].astype(BF16)
        send(xsend.at[s, pl.ds(half, half)], xland.at[s, pl.ds(half, half)], rs_s.at[4, s], rs_r.at[4, s], X)
        ysend[s, pl.ds(0, half)] = cont[s, at_half(jy, 0)].astype(BF16)
        send(ysend.at[s, pl.ds(0, half)], yland.at[s, pl.ds(0, half)], rs_s.at[5, s], rs_r.at[5, s], Y)

    def reduce_first(s):
        landed(dland.at[s, pl.ds(0, half)], rs_s.at[0, s], rs_r.at[0, s], Y)
        xsend[s, pl.ds(0, half)] = (
            cont[s, at_half(jx, 0)] + dland[s, pl.ds(0, half)].astype(F32)
        ).astype(BF16)
        send(xsend.at[s, pl.ds(0, half)], xland.at[s, pl.ds(0, half)], rs_s.at[2, s], rs_r.at[2, s], X)
        landed(dland.at[s, pl.ds(half, half)], rs_s.at[1, s], rs_r.at[1, s], X)
        ysend[s, pl.ds(half, half)] = (
            cont[s, at_half(jy, 1)] + dland[s, pl.ds(half, half)].astype(F32)
        ).astype(BF16)
        send(ysend.at[s, pl.ds(half, half)], yland.at[s, pl.ds(half, half)], rs_s.at[3, s], rs_r.at[3, s], Y)

    def reduce_second(s):
        landed(xland.at[s, pl.ds(half, half)], rs_s.at[4, s], rs_r.at[4, s], X)
        landed(yland.at[s, pl.ds(0, half)], rs_s.at[5, s], rs_r.at[5, s], Y)
        landed(xland.at[s, pl.ds(0, half)], rs_s.at[2, s], rs_r.at[2, s], X)
        landed(yland.at[s, pl.ds(half, half)], rs_s.at[3, s], rs_r.at[3, s], Y)
        total = cont[s, at_rows(j)] + xland[s].astype(F32) + yland[s].astype(F32)
        if s == 0:
            acc[...] = total
        else:
            zsend[s] = total.astype(BF16)
            send(zsend.at[s], zland.at[z], z_s.at[s], z_r.at[z], {"dp": peers[s - 1]})

    spread_xy(0)
    for i in range(1, LINE):
        send(ext, tok.at[at_rows(me)], col_s.at[i - 1], col_r.at[z], {"dp": peers[i - 1]})
    for c in weight_copies:
        c.start()
    half_forward(0)
    column_forward(1)
    half_forward(1)
    column_forward(2)
    own_copy.wait()
    order = list(range(1, LINE)) + [0]
    for k, s in enumerate(order):
        diag_wait(s)
        if k == 0:
            weight_copies[0].wait()
            weight_copies[1].wait()
        project(s, 1 - core, psend.at[s])
        send(psend.at[s], precv.at[s], ep_s.at[0, s], ep_r.at[0, s], E)
        project(s, core, pown)
        hide(s)
        if k + 2 < LINE:
            half_forward(k + 2)
        if k + 3 < LINE:
            column_forward(k + 3)
        if k >= 1:
            reduce_first(order[k - 1])
        if k >= 2:
            reduce_second(order[k - 2])
        if k == 0:
            weight_copies[2].wait()
        lower(s)
    reduce_second(order[-2])
    reduce_first(order[-1])
    reduce_second(order[-1])
    total = acc[...]
    for s in range(1, LINE):
        landed(zland.at[plane[s]], z_s.at[s], z_r.at[plane[s]], X)
        total += zland[plane[s]].astype(F32)
    out[...] = total.astype(BF16)
    for c in started:
        c.wait_send()


def fused(tokens, gate_weight, up_weight, down_weight, targets, mixing, move_plan):
    groups = lax.axis_size("dp")
    rows, wide = tokens.shape
    lanes = jnp.arange(groups, dtype=jnp.int32)
    share = share_of(targets, mixing, move_plan, lanes)
    high = lax.reduce_precision(share, 8, 7)
    middle = lax.reduce_precision(share - high, 8, 7)
    low = share - high - middle
    pad = -(3 * groups) % 128
    ext = jnp.concatenate(
        [tokens, high.astype(BF16), middle.astype(BF16), low.astype(BF16), jnp.zeros((rows, pad), BF16)],
        axis=1,
    )
    full = gate_weight.shape[2]
    keep = full // lax.axis_size("ep")
    block = PLANE * rows
    VM, DMA = pltpu.VMEM, pltpu.SemaphoreType.DMA
    return pl.pallas_call(
        functools.partial(kernel, groups),
        out_shape=jax.ShapeDtypeStruct((rows, wide), BF16),
        in_specs=[pl.BlockSpec(memory_space=pltpu.VMEM)] + [pl.BlockSpec(memory_space=pl.ANY)] * 3,
        out_specs=pl.BlockSpec(memory_space=pltpu.VMEM),
        scratch_shapes=[
            VM((wide, full), BF16), VM((wide, full), BF16), VM((full, wide), BF16),
            VM((groups * rows, ext.shape[1]), BF16),
            VM((LINE, block, 2 * keep), F32), VM((LINE, block, 2 * keep), F32),
            VM((block, 2 * keep), F32), VM((LINE, 2, block, keep), BF16),
            VM((LINE, block, wide), F32),
            VM((LINE, rows, wide), BF16), VM((LINE, rows, wide), BF16),
            VM((LINE, rows, wide), BF16), VM((LINE, rows, wide), BF16),
            VM((LINE, rows, wide), BF16), VM((LINE, rows, wide), BF16),
            VM((LINE, rows, wide), BF16), VM((LINE, rows, wide), BF16),
            VM((rows, wide), F32),
            DMA((3,)), DMA((1,)), DMA((LINE - 1,)), DMA((LINE,)),
            DMA((4, LINE)), DMA((4, LINE)), DMA((2, LINE)), DMA((2, LINE)),
            DMA((6, LINE)), DMA((6, LINE)), DMA((LINE,)), DMA((LINE,)),
        ],
        compiler_params=pltpu.CompilerParams(
            collective_id=0, has_side_effects=True, vmem_limit_bytes=63 * 1024 * 1024
        ),
    )(ext, gate_weight[0], up_weight[0], down_weight[0])


def plain(tokens, gate_weight, up_weight, down_weight, targets, mixing, move_plan):
    groups = lax.axis_size("dp")
    me = lax.axis_index("dp")
    lanes = jnp.arange(groups, dtype=jnp.int32)
    share = share_of(targets, mixing, move_plan, lanes)
    shares = lax.all_gather(share, "dp", axis=0, tiled=True)
    rows = lax.all_gather(tokens, "dp", axis=0, tiled=True)
    width = rows.shape[0]
    dims = (((0,), (1,)), ((), ()))
    gate_term = lax.dot_general(gate_weight[0], rows, dims, preferred_element_type=F32)
    up_term = lax.dot_general(up_weight[0], rows, dims, preferred_element_type=F32)
    summed = lax.psum_scatter(
        jnp.concatenate([gate_term, up_term], axis=1), "ep", scatter_dimension=0, tiled=True
    )
    hidden = (jax.nn.silu(summed[:, :width]) * summed[:, width:]).astype(BF16)
    output = lax.dot_general(
        lax.all_gather(hidden, "ep", axis=0, tiled=True),
        down_weight[0],
        (((0,), (0,)), ((), ())),
        preferred_element_type=F32,
    )
    scale = jnp.sum(jnp.where(lanes == me, shares, 0.0), axis=1, keepdims=True)
    scaled = output.astype(BF16).astype(F32) * scale
    return lax.psum_scatter(scaled.astype(BF16), "dp", scatter_dimension=0, tiled=True)


def solution(mesh):
    small = mesh.shape["dp"] == PLANE * LINE and mesh.shape["ep"] == 2
    return jax.shard_map(
        fused if small else plain,
        mesh=mesh,
        in_specs=(
            P("dp", "ep"),
            P("dp", "ep", None),
            P("dp", "ep", None),
            P("dp", None, "ep"),
            P("dp", None),
            P("dp", None),
            P(),
        ),
        out_specs=P("dp", "ep"),
        check_vma=False,
    )
```
